512 devices in a mesh: seq: 64 (over z, y), ch: 8 (over x, core).
Axes of the slice: x: 4, y: 4, z: 16, core: 2. Of those that a mesh axis runs over, the one named last changes fastest.
Arguments:
- query_branch: bfloat16 [16384, 2048], P('seq', 'ch'), may hold values from -6 to 6
- key_branch: bfloat16 [16384, 2048], P('seq', 'ch'), may hold values from -6 to 6
- value_branch: bfloat16 [16384, 2048], P('seq', 'ch'), may hold values from -6 to 6
- short_taps: float32 [3, 7, 2048], P(None, None, 'ch'), may hold values from -2 to 2
- long_taps: float32 [16384, 2048], P('seq', 'ch'), may hold values from -1.5 to 1.5
- skip_gain: float32 [2048], P('ch'), may hold values from 0.5 to 2
Outputs:
- gated_output: bfloat16 [16384, 2048], P('seq', 'ch')
The draws below stay inside these ranges and needn't reach their ends.
All inputs are finite; a program needn't handle non-finite values.
Results may differ from the reference program's by a relative error of at most 0.001.
Values may be sent and summed in bfloat16 or wider, within the bound.
No kernel may reach another device: no remote copies, remote signals or barrier semaphores. Data moves between devices by JAX's collectives and lax.ppermute only.
A program may use at most 64 MiB of HBM per device.

```python
import math
import jax
import jax.numpy as jnp
from jax import lax

KERNEL = 7
SEQ = 16384
CHANNELS = 2048


def envelope_scale(rates, share):
    return jnp.sqrt(share * 2.0 * rates / -jnp.expm1(-2.0 * rates * SEQ))


def draw_long_taps(key, part):
    keys = jax.random.split(key, 7)
    positions = jnp.arange(SEQ, dtype=jnp.float32)[:, None]
    rate_low = jnp.log(0.5 / SEQ)
    rate_high = jnp.log(1.0 / 32.0)
    rates = jnp.exp(jax.random.uniform(keys[0], (CHANNELS,), jnp.float32, rate_low, rate_high))
    rough_part = jnp.clip(jax.random.normal(keys[1], (SEQ, CHANNELS), jnp.float32), -5.0, 5.0)
    tail_rates = jnp.exp(jax.random.uniform(keys[4], (CHANNELS,), jnp.float32, jnp.log(0.1 / SEQ), jnp.log(1.0 / SEQ)))
    tail_rough = jnp.clip(jax.random.normal(keys[5], (SEQ, CHANNELS), jnp.float32), -5.0, 5.0)
    tail_share = jax.random.uniform(keys[6], (CHANNELS,), jnp.float32, 0.1, 0.3)
    head = rough_part * envelope_scale(rates, 1.0 - tail_share) * jnp.exp(-rates * positions)
    tail = tail_rough * envelope_scale(tail_rates, tail_share) * jnp.exp(-tail_rates * positions)
    return (head + tail).astype(jnp.float32)


def block_levels(key, shape, cuts, low, top_value):
    def one(axis_at, shards_of):
        draws = jax.random.uniform(jax.random.fold_in(jax.random.fold_in(key, 6), axis_at), (shards_of,), jnp.float32, low / len(cuts), top_value / len(cuts))
        return jnp.repeat(jnp.exp(draws), shape[axis_at] // shards_of).reshape((-1,) + (1,) * (len(shape) - axis_at - 1))

    loudness = one(*cuts[0])
    for cut in cuts[1:]:
        loudness = loudness * one(*cut)
    return loudness


def normal_values(rng, extent, width, bound, shards=(), held_as=jnp.bfloat16):
    factor_of = block_levels(rng, extent, shards, -0.22, 0.18) if shards else 1.0
    drawn = jax.random.normal(rng, extent, jnp.float32) * width * factor_of
    return jnp.minimum(jnp.maximum(drawn, -bound), bound).astype(held_as)


def setup_inputs(seed: int = 0) -> dict:
    seeds = jax.random.split(jax.random.key(seed), 7)
    query_branch = normal_values(seeds[0], (SEQ, CHANNELS), 1.0, 6.0, ((0, 64), (1, 8)))
    key_branch = normal_values(seeds[1], (SEQ, CHANNELS), 1.0, 6.0, ((0, 64), (1, 8)))
    value_branch = normal_values(seeds[2], (SEQ, CHANNELS), 1.0, 6.0, ((0, 64), (1, 8)))
    short_taps = normal_values(seeds[3], (3, KERNEL, CHANNELS), KERNEL ** -0.5, 2.0, ((2, 8),), jnp.float32)
    long_taps = draw_long_taps(jax.random.fold_in(seeds[6], 71), 0)
    skip_gain = jnp.clip(0.5 + 1.5 * jax.random.uniform(seeds[5], (CHANNELS,), jnp.float32) ** block_levels(seeds[5], (CHANNELS,), ((0, 8),), -0.2, 0.2), 0.5, 2.0)
    return {"query_branch": query_branch, "key_branch": key_branch, "value_branch": value_branch, "short_taps": short_taps, "long_taps": long_taps, "skip_gain": skip_gain}


def short_filter(values, weights):
    row_count = values.shape[0]
    margin = weights.shape[0] - 1
    padded = jnp.concatenate([jnp.zeros((margin, values.shape[1]), jnp.float32), values.astype(jnp.float32)], axis=0)
    total = weights[0] * padded[:row_count]
    for offset in range(1, weights.shape[0]):
        total = total + weights[offset] * padded[offset:offset + row_count]
    return total


def causal_filter(signal, weights):
    row_count, channels = signal.shape
    group_size = math.gcd(channels, 64)
    groups = channels // group_size
    signal_groups = signal.reshape(row_count, groups, group_size).transpose(1, 0, 2)
    weight_groups = weights.reshape(row_count, groups, group_size).transpose(1, 0, 2)

    def single(couple):
        spectrum = jnp.fft.rfft(couple[0], n=2 * row_count, axis=0) * jnp.fft.rfft(couple[1], n=2 * row_count, axis=0)
        return jnp.fft.irfft(spectrum, n=2 * row_count, axis=0)[:row_count]

    result = lax.map(single, (signal_groups, weight_groups))
    return result.transpose(1, 0, 2).reshape(row_count, channels)


def reference(query_branch, key_branch, value_branch, short_taps, long_taps, skip_gain):
    query_mix = short_filter(query_branch, short_taps[0])
    key_mix = short_filter(key_branch, short_taps[1])
    value_mix = short_filter(value_branch, short_taps[2])
    gated_in = key_mix * value_mix
    long_mix = causal_filter(gated_in, long_taps)
    return (query_mix * (long_mix + skip_gain * gated_in)).astype(jnp.bfloat16)
```

```python
import jax
import jax.numpy as jnp
import numpy as np
from jax import lax
from jax.experimental import pallas as pl
from jax.experimental.pallas import tpu as pltpu
from jax.sharding import PartitionSpec as P

f32 = jnp.float32
bf16 = jnp.bfloat16

BLOCKS = 64
ROWS = 256
OWN = 4
TOTAL = BLOCKS * ROWS
TAPS = 7


def halves(table):
    high = table.astype(jnp.bfloat16)
    low = (table - high.astype(np.float64)).astype(jnp.bfloat16)
    return high, low


def make_tables():
    turn = 2.0 * np.pi
    freq = np.arange(BLOCKS) + 0.25
    block = np.arange(BLOCKS)
    row = np.arange(ROWS)
    angle = turn * freq[:, None] * block[None, :] / BLOCKS
    high, low = halves(np.concatenate([np.cos(angle), -np.sin(angle)], axis=0))
    outer = np.concatenate([high, low, high], axis=1)
    high, low = halves(np.concatenate([np.cos(angle.T), -np.sin(angle.T)], axis=1) / TOTAL)
    outer_back = np.concatenate([high, low, high], axis=1)
    angle = turn * freq[:, None] * row[None, :] / TOTAL
    twist = np.stack([np.cos(angle), -np.sin(angle)]).astype(np.float32)
    angle = turn * (row[:, None] * row[None, :] % ROWS) / ROWS
    inner = np.stack(halves(np.concatenate([np.cos(angle), np.sin(angle)], axis=1)))
    return outer, outer_back, twist, inner


def split(value):
    high = value.astype(bf16)
    return high, (value - high.astype(f32)).astype(bf16)


def dot(left, right):
    return jnp.dot(left, right, preferred_element_type=f32)


def pack_kernel(key_ref, value_ref, long_ref, out_ref, stage_ref):
    long_t = long_ref[...].T
    long_high = long_t.astype(bf16).astype(f32)
    parts = (key_ref[...].astype(f32).T, value_ref[...].astype(f32).T, long_high, long_t - long_high)
    for place, part in enumerate(parts):
        for own in range(OWN):
            stage_ref[:, place * OWN + own, :] = part[own * BLOCKS : (own + 1) * BLOCKS]
    out_ref[...] = stage_ref[...].astype(bf16)


def filter_kernel(
    got_ref, taps_ref, gain_ref, outer_ref, back_ref, twist_ref, inner_ref, out_ref, stage_ref
):
    stage_ref[...] = got_ref[...].astype(f32)
    lane = lax.broadcasted_iota(jnp.int32, (BLOCKS, ROWS), 1)
    first = lax.broadcasted_iota(jnp.int32, (BLOCKS, ROWS), 0) == 0

    def short(value, branch, own):
        before = jnp.where(first, 0.0, pltpu.roll(value, 1, 0))
        total = taps_ref[branch, TAPS - 1, own] * value
        for back in range(1, TAPS):
            moved = pltpu.roll(jnp.where(lane >= ROWS - back, before, value), back, 1)
            total = total + taps_ref[branch, TAPS - 1 - back, own] * moved
        return total

    gated = []
    for own in range(OWN):
        key_mix = short(stage_ref[:, own, :], 0, own)
        value_mix = short(stage_ref[:, OWN + own, :], 1, own)
        gated.append(key_mix * value_mix)
    signal_high, signal_low = split(jnp.concatenate(gated, axis=1))
    long_high = jnp.concatenate(
        [stage_ref[:, 2 * OWN + own, :] for own in range(OWN)], axis=1
    ).astype(bf16)
    long_low = jnp.concatenate(
        [stage_ref[:, 3 * OWN + own, :] for own in range(OWN)], axis=1
    ).astype(bf16)
    twist_real = twist_ref[0]
    twist_imag = twist_ref[1]
    inner_high = inner_ref[0]
    inner_low = inner_ref[1]

    def inner_product(value):
        high, low = split(value)
        return dot(high, inner_high) + dot(high, inner_low) + dot(low, inner_high)

    def spectrum(high, low):
        across = dot(outer_ref[...], jnp.concatenate([high, high, low], axis=0))
        real = []
        imag = []
        for own in range(OWN):
            piece_real = across[:BLOCKS, own * ROWS : (own + 1) * ROWS]
            piece_imag = across[BLOCKS:, own * ROWS : (own + 1) * ROWS]
            real.append(piece_real * twist_real - piece_imag * twist_imag)
            imag.append(piece_real * twist_imag + piece_imag * twist_real)
        both = inner_product(jnp.concatenate(real + imag, axis=0))
        half = OWN * BLOCKS
        return (
            both[:half, :ROWS] + both[half:, ROWS:],
            both[half:, :ROWS] - both[:half, ROWS:],
        )

    signal_real, signal_imag = spectrum(signal_high, signal_low)
    long_real, long_imag = spectrum(long_high, long_low)
    prod_real = signal_real * long_real - signal_imag * long_imag
    prod_imag = signal_real * long_imag + signal_imag * long_real
    both = inner_product(jnp.concatenate([prod_real, prod_imag], axis=0))
    half = OWN * BLOCKS
    time_real = both[:half, :ROWS] - both[half:, ROWS:]
    time_imag = both[half:, :ROWS] + both[:half, ROWS:]
    real = []
    imag = []
    for own in range(OWN):
        piece_real = time_real[own * BLOCKS : (own + 1) * BLOCKS]
        piece_imag = time_imag[own * BLOCKS : (own + 1) * BLOCKS]
        real.append(piece_real * twist_real + piece_imag * twist_imag)
        imag.append(piece_imag * twist_real - piece_real * twist_imag)
    high, low = split(
        jnp.concatenate([jnp.concatenate(real, axis=1), jnp.concatenate(imag, axis=1)], axis=0)
    )
    mixed = dot(back_ref[...], jnp.concatenate([high, high, low], axis=0))
    for own in range(OWN):
        total = mixed[:, own * ROWS : (own + 1) * ROWS] + gain_ref[own] * gated[own]
        out_ref[:, 2 * own, :] = total[:, : ROWS // 2]
        out_ref[:, 2 * own + 1, :] = total[:, ROWS // 2 :]


def finish_kernel(got_ref, query_ref, out_ref):
    rows = []
    for own in range(OWN):
        rows.append(jnp.concatenate([got_ref[:, 2 * own, :], got_ref[:, 2 * own + 1, :]], axis=1))
    out_ref[...] = (query_ref[...] * jnp.concatenate(rows, axis=0).T).astype(bf16)


def in_vmem(count):
    return [pl.BlockSpec(memory_space=pltpu.VMEM)] * count


def short_filter(values, rim_part, weights):
    row_count = values.shape[0]
    padded = jnp.concatenate([rim_part, values], axis=0).astype(f32)
    total = weights[0] * padded[:row_count]
    for offset in range(1, weights.shape[0]):
        total = total + weights[offset] * padded[offset : offset + row_count]
    return total


def shards(query_branch, key_branch, value_branch, short_taps, long_taps, skip_gain):
    outer, outer_back, twist, inner = make_tables()
    packed = pl.pallas_call(
        pack_kernel,
        out_shape=jax.ShapeDtypeStruct((BLOCKS, 4 * OWN, ROWS), bf16),
        in_specs=in_vmem(3),
        out_specs=in_vmem(1)[0],
        scratch_shapes=[pltpu.VMEM((BLOCKS, 4 * OWN, ROWS), f32)],
        name="pack",
    )(key_branch, value_branch, long_taps)
    got = lax.all_to_all(packed, "seq", split_axis=0, concat_axis=0, tiled=True)
    place = lax.axis_index("seq")
    own_taps = lax.dynamic_index_in_dim(
        short_taps[1:].reshape(2, TAPS, OWN, BLOCKS), place, 3, keepdims=False
    )
    own_gain = lax.dynamic_index_in_dim(skip_gain.reshape(OWN, BLOCKS), place, 1, keepdims=False)
    mixed = pl.pallas_call(
        filter_kernel,
        out_shape=jax.ShapeDtypeStruct((BLOCKS, 2 * OWN, ROWS // 2), f32),
        in_specs=in_vmem(1) + [pl.BlockSpec(memory_space=pltpu.SMEM)] * 2 + in_vmem(4),
        out_specs=in_vmem(1)[0],
        scratch_shapes=[pltpu.VMEM((BLOCKS, 4 * OWN, ROWS), f32)],
        name="filter",
    )(got, own_taps, own_gain, outer, outer_back, twist, inner)
    back = lax.all_to_all(mixed, "seq", split_axis=0, concat_axis=0, tiled=True)
    rim = lax.ppermute(
        query_branch[-(TAPS - 1) :], "seq", [(i, i + 1) for i in range(BLOCKS - 1)]
    )
    query_mix = short_filter(query_branch, rim, short_taps[0])
    return pl.pallas_call(
        finish_kernel,
        out_shape=jax.ShapeDtypeStruct(query_branch.shape, bf16),
        in_specs=in_vmem(2),
        out_specs=in_vmem(1)[0],
        name="finish",
    )(back, query_mix)


def solution(mesh):
    return jax.shard_map(
        shards,
        mesh=mesh,
        in_specs=(
            P("seq", "ch"),
            P("seq", "ch"),
            P("seq", "ch"),
            P(None, None, "ch"),
            P("seq", "ch"),
            P("ch"),
        ),
        out_specs=P("seq", "ch"),
        check_vma=False,
    )
```

```python
import jax
import jax.numpy as jnp
import numpy as np
from jax import lax
from jax.experimental import pallas as pl
from jax.experimental.pallas import tpu as pltpu
from jax.sharding import PartitionSpec as P

f32 = jnp.float32
bf16 = jnp.bfloat16

BLOCKS = 64
ROWS = 256
OWN = 4
TOTAL = BLOCKS * ROWS
TAPS = 7
LANES = ROWS // 2
SENT = 6 * OWN
BACK = 2 * OWN
HOLD = 7000
SIDE_LEN = 8
LEAD = 42
LEAD_BACK = 34
TURN = (LEAD_BACK - LEAD) // SIDE_LEN % SIDE_LEN


def order(lead):
    place = [rank % SIDE_LEN * SIDE_LEN + rank // SIDE_LEN for rank in range(BLOCKS)]
    return [(at + lead) % BLOCKS for at in place]


START_GROUP = -LEAD % SIDE_LEN
START_ROW = -LEAD % BLOCKS // SIDE_LEN

FLOOR = 2.0**-10
CODE_LOW = -125.0
CODE_RATE = 250.0 / np.log2(1.0 + 1.6 / FLOOR)


def halves(table):
    high = table.astype(jnp.bfloat16)
    low = (table - high.astype(np.float64)).astype(jnp.bfloat16)
    return high, low


def make_tables():
    turn = 2.0 * np.pi
    freq = np.arange(BLOCKS) + 0.25
    row = np.arange(ROWS)
    angle = turn * freq[:, None] * np.array(order(LEAD))[None, :] / BLOCKS
    high, low = halves(np.concatenate([np.cos(angle), -np.sin(angle)], axis=0))
    outer = np.concatenate([high, low, high], axis=1)
    angle = turn * freq[:, None] * np.array(order(LEAD_BACK))[None, :] / BLOCKS
    high, low = halves(np.concatenate([np.cos(angle.T), -np.sin(angle.T)], axis=1) / TOTAL)
    outer_back = np.concatenate([high, low, high], axis=1)
    angle = turn * freq[:, None] * row[None, :] / TOTAL
    twist = np.stack([np.cos(angle), -np.sin(angle)]).astype(np.float32)
    angle = turn * (row[:, None] * row[None, :] % ROWS) / ROWS
    inner = np.stack(halves(np.concatenate([np.cos(angle), np.sin(angle)], axis=1)))
    return outer, outer_back, twist, inner


def split(value):
    high = value.astype(bf16)
    return high, (value - high.astype(f32)).astype(bf16)


def turned(value, shift):
    groups = value.reshape(BLOCKS // SIDE_LEN, SIDE_LEN, LANES)
    return pltpu.roll(groups, shift % SIDE_LEN, 1).reshape(BLOCKS, LANES)


def dot(left, right):
    return jnp.dot(left, right, preferred_element_type=f32)


def encode(value):
    code = jnp.exp2(CODE_RATE * jnp.log2(1.0 + jnp.abs(value) * (1.0 / FLOOR)) + CODE_LOW)
    return jnp.where(value < 0.0, -code, code)


def decode(code):
    size = (jnp.exp2((jnp.log2(jnp.abs(code)) - CODE_LOW) * (1.0 / CODE_RATE)) - 1.0) * FLOOR
    return jnp.where(code < 0.0, -size, size)


def pack_kernel(hold_ref, key_ref, value_ref, long_ref, out_ref, stage_ref):
    parts = (
        key_ref[...].astype(f32).T,
        value_ref[...].astype(f32).T,
        encode(long_ref[...]).T,
    )
    for place, part in enumerate(parts):
        for own in range(OWN):
            piece = part[own * BLOCKS : (own + 1) * BLOCKS]
            row = 2 * (place * OWN + own)
            stage_ref[pl.ds(row, BLOCKS, stride=SENT), :] = piece[:, :LANES]
            stage_ref[pl.ds(row + 1, BLOCKS, stride=SENT), :] = piece[:, LANES:]
    out_ref[...] = stage_ref[...].astype(bf16)
    pl.delay(hold_ref[0])


def filter_kernel(
    got_ref, taps_ref, gain_ref, outer_ref, back_ref, twist_ref, inner_ref, out_ref, stage_ref
):
    stage_ref[...] = got_ref[...].astype(f32)
    twist_real = twist_ref[0]
    twist_imag = twist_ref[1]
    inner_high = inner_ref[0]
    inner_low = inner_ref[1]
    half = OWN * BLOCKS

    def staged(row):
        return stage_ref[pl.ds(row, BLOCKS, stride=SENT), :]

    def inner_product(value):
        high, low = split(value)
        return dot(high, inner_high) + dot(high, inner_low) + dot(low, inner_high)

    def spectrum(signal):
        high, low = split(signal)
        across = dot(outer_ref[...], jnp.concatenate([high, high, low], axis=0))
        real = []
        imag = []
        for own in range(OWN):
            piece_real = across[:BLOCKS, own * ROWS : (own + 1) * ROWS]
            piece_imag = across[BLOCKS:, own * ROWS : (own + 1) * ROWS]
            real.append(piece_real * twist_real - piece_imag * twist_imag)
            imag.append(piece_real * twist_imag + piece_imag * twist_real)
        both = inner_product(jnp.concatenate(real + imag, axis=0))
        return (
            both[:half, :ROWS] + both[half:, ROWS:],
            both[half:, :ROWS] - both[:half, ROWS:],
        )

    first_row = 4 * OWN
    long_real, long_imag = spectrum(
        decode(jnp.concatenate([staged(first_row + i) for i in range(2 * OWN)], axis=1))
    )

    lane = lax.broadcasted_iota(jnp.int32, (BLOCKS, LANES), 1)
    first = lax.broadcasted_iota(jnp.int32, (SIDE_LEN, LANES), 0) == START_ROW

    def short(branch, own):
        early = staged(2 * (branch * OWN + own))
        late = staged(2 * (branch * OWN + own) + 1)
        groups = [pltpu.roll(late[-SIDE_LEN:], 1, 0)]
        groups += [late[i : i + SIDE_LEN] for i in range(0, BLOCKS - SIDE_LEN, SIDE_LEN)]
        groups[START_GROUP] = jnp.where(first, 0.0, groups[START_GROUP])
        tap = taps_ref[branch, TAPS - 1, own]
        early_sum = tap * early
        late_sum = tap * late
        for back in range(1, TAPS):
            tap = taps_ref[branch, TAPS - 1 - back, own]
            moved_early = pltpu.roll(early, back, 1)
            moved_late = pltpu.roll(late, back, 1)
            moved_before = [
                pltpu.roll(group, back, 1)
                if i in (0, START_GROUP)
                else moved_late[(i - 1) * SIDE_LEN : i * SIDE_LEN]
                for i, group in enumerate(groups)
            ]
            moved_before = jnp.concatenate(moved_before, axis=0)
            early_sum = early_sum + tap * jnp.where(lane < back, moved_before, moved_early)
            late_sum = late_sum + tap * jnp.where(lane < back, moved_early, moved_late)
        return early_sum, late_sum

    gated = []
    for own in range(OWN):
        for key_mix, value_mix in zip(short(0, own), short(1, own)):
            gated.append(key_mix * value_mix)
    signal_real, signal_imag = spectrum(jnp.concatenate(gated, axis=1))
    prod_real = signal_real * long_real - signal_imag * long_imag
    prod_imag = signal_real * long_imag + signal_imag * long_real
    both = inner_product(jnp.concatenate([prod_real, prod_imag], axis=0))
    time_real = both[:half, :ROWS] - both[half:, ROWS:]
    time_imag = both[half:, :ROWS] + both[:half, ROWS:]
    real = []
    imag = []
    for own in range(OWN):
        piece_real = time_real[own * BLOCKS : (own + 1) * BLOCKS]
        piece_imag = time_imag[own * BLOCKS : (own + 1) * BLOCKS]
        real.append(piece_real * twist_real + piece_imag * twist_imag)
        imag.append(piece_imag * twist_real - piece_real * twist_imag)
    high, low = split(
        jnp.concatenate([jnp.concatenate(real, axis=1), jnp.concatenate(imag, axis=1)], axis=0)
    )
    mixed = dot(back_ref[...], jnp.concatenate([high, high, low], axis=0))
    for i in range(2 * OWN):
        out_ref[pl.ds(i, BLOCKS, stride=BACK), :] = (
            mixed[:, i * LANES : (i + 1) * LANES] + gain_ref[i // 2] * turned(gated[i], -TURN)
        )


def finish_kernel(got_ref, query_ref, out_ref):
    rows = []
    for own in range(OWN):
        early = got_ref[pl.ds(2 * own, BLOCKS, stride=BACK), :]
        late = got_ref[pl.ds(2 * own + 1, BLOCKS, stride=BACK), :]
        rows.append(jnp.concatenate([turned(early, TURN), turned(late, TURN)], axis=1))
    out_ref[...] = (query_ref[...] * jnp.concatenate(rows, axis=0).T).astype(bf16)


def in_vmem(count):
    return [pl.BlockSpec(memory_space=pltpu.VMEM)] * count


def short_filter(values, rim_part, weights):
    row_count = values.shape[0]
    padded = jnp.concatenate([rim_part, values], axis=0).astype(f32)
    total = weights[0] * padded[:row_count]
    for offset in range(1, weights.shape[0]):
        total = total + weights[offset] * padded[offset : offset + row_count]
    return total


def near(value):
    return pltpu.with_memory_space_constraint(value, pltpu.VMEM)


def exchange(blocks, lead):
    moved = lax.all_to_all(
        blocks.reshape(BLOCKS, -1, LANES),
        "seq",
        split_axis=0,
        concat_axis=0,
        axis_index_groups=[order(lead)],
        tiled=True,
    )
    return moved.reshape(blocks.shape)


def shards(query_branch, key_branch, value_branch, short_taps, long_taps, skip_gain):
    outer, outer_back, twist, inner = make_tables()
    rim = lax.ppermute(
        query_branch[-(TAPS - 1) :], "seq", [(i, i + 1) for i in range(BLOCKS - 1)]
    )
    query_mix = short_filter(query_branch, rim, short_taps[0])
    hold = jnp.full((1,), HOLD * (1 - lax.axis_index("ch") % 2), jnp.int32)
    packed = pl.pallas_call(
        pack_kernel,
        out_shape=pltpu.VMEM((BLOCKS * SENT, LANES), bf16),
        in_specs=[pl.BlockSpec(memory_space=pltpu.SMEM)] + in_vmem(3),
        out_specs=in_vmem(1)[0],
        scratch_shapes=[pltpu.VMEM((BLOCKS * SENT, LANES), f32)],
        name="pack",
    )(hold, key_branch, value_branch, long_taps)
    got = exchange(packed, LEAD)
    got, query_mix = lax.optimization_barrier((got, query_mix))
    place = (lax.axis_index("seq") + BLOCKS - LEAD) % BLOCKS
    place = place % SIDE_LEN * SIDE_LEN + place // SIDE_LEN
    own_taps = lax.dynamic_index_in_dim(
        short_taps[1:].reshape(2, TAPS, OWN, BLOCKS), place, 3, keepdims=False
    )
    own_gain = lax.dynamic_index_in_dim(skip_gain.reshape(OWN, BLOCKS), place, 1, keepdims=False)
    mixed = pl.pallas_call(
        filter_kernel,
        out_shape=pltpu.VMEM((BLOCKS * BACK, LANES), f32),
        in_specs=in_vmem(1) + [pl.BlockSpec(memory_space=pltpu.SMEM)] * 2 + in_vmem(4),
        out_specs=in_vmem(1)[0],
        scratch_shapes=[pltpu.VMEM((BLOCKS * SENT, LANES), f32)],
        name="filter",
    )(near(got), own_taps, own_gain, near(outer), near(outer_back), near(twist), near(inner))
    back = exchange(mixed, LEAD_BACK)
    return pl.pallas_call(
        finish_kernel,
        out_shape=jax.ShapeDtypeStruct(query_branch.shape, bf16),
        in_specs=in_vmem(2),
        out_specs=in_vmem(1)[0],
        name="finish",
    )(near(back), near(query_mix))


def solution(mesh):
    return jax.shard_map(
        shards,
        mesh=mesh,
        in_specs=(
            P("seq", "ch"),
            P("seq", "ch"),
            P("seq", "ch"),
            P(None, None, "ch"),
            P("seq", "ch"),
            P("ch"),
        ),
        out_specs=P("seq", "ch"),
        check_vma=False,
    )
```

```python
import jax
import jax.numpy as jnp
import numpy as np
from jax import lax
from jax.experimental import pallas as pl
from jax.experimental.pallas import tpu as pltpu
from jax.sharding import PartitionSpec as P

f32 = jnp.float32
bf16 = jnp.bfloat16

BLOCKS = 64
ROWS = 256
OWN = 4
TOTAL = BLOCKS * ROWS
TAPS = 7
LANES = ROWS // 2
SENT = 6 * OWN
BACK = 2 * OWN + 2
HOLD = 7000
SIDE_LEN = 8
LEAD = 42
LEAD_BACK = 34
TURN = (LEAD_BACK - LEAD) // SIDE_LEN % SIDE_LEN


def order(lead):
    place = [rank % SIDE_LEN * SIDE_LEN + rank // SIDE_LEN for rank in range(BLOCKS)]
    return [(at + lead) % BLOCKS for at in place]


START_GROUP = -LEAD % SIDE_LEN
START_ROW = -LEAD % BLOCKS // SIDE_LEN

FLOOR = 2.0**-10
CODE_LOW = -125.0
CODE_RATE = 250.0 / np.log2(1.0 + 1.6 / FLOOR)


def halves(table):
    high = table.astype(jnp.bfloat16)
    low = (table - high.astype(np.float64)).astype(jnp.bfloat16)
    return high, low


def make_tables():
    turn = 2.0 * np.pi
    freq = np.arange(BLOCKS) + 0.25
    row = np.arange(ROWS)
    angle = turn * freq[:, None] * np.array(order(LEAD))[None, :] / BLOCKS
    high, low = halves(np.concatenate([np.cos(angle), -np.sin(angle)], axis=0))
    outer = np.concatenate([high, low, high], axis=1)
    angle = turn * freq[:, None] * np.array(order(LEAD_BACK))[None, :] / BLOCKS
    high, low = halves(np.concatenate([np.cos(angle.T), -np.sin(angle.T)], axis=1) / TOTAL)
    outer_back = np.concatenate([high, low, high], axis=1)
    angle = turn * freq[:, None] * row[None, :] / TOTAL
    twist = np.stack([np.cos(angle), -np.sin(angle)]).astype(np.float32)
    angle = turn * (row[:, None] * row[None, :] % ROWS) / ROWS
    inner = np.stack(halves(np.concatenate([np.cos(angle), np.sin(angle)], axis=1)))
    return outer, outer_back, twist, inner


def split(value):
    high = value.astype(bf16)
    return high, (value - high.astype(f32)).astype(bf16)


def turned(value, shift):
    groups = value.reshape(BLOCKS // SIDE_LEN, SIDE_LEN, LANES)
    return pltpu.roll(groups, shift % SIDE_LEN, 1).reshape(BLOCKS, LANES)


def dot(left, right):
    return jnp.dot(left, right, preferred_element_type=f32)


def encode(value):
    code = jnp.exp2(CODE_RATE * jnp.log2(1.0 + jnp.abs(value) * (1.0 / FLOOR)) + CODE_LOW)
    return jnp.where(value < 0.0, -code, code)


def decode(code):
    size = (jnp.exp2((jnp.log2(jnp.abs(code)) - CODE_LOW) * (1.0 / CODE_RATE)) - 1.0) * FLOOR
    return jnp.where(code < 0.0, -size, size)


def encode_scaled(value, scale):
    code = jnp.exp2(jnp.abs(value) * (-2.0 * CODE_LOW / scale) + CODE_LOW)
    return jnp.where(value < 0.0, -code, code)


def decode_scaled(code, scale):
    size = (jnp.log2(jnp.abs(code)) - CODE_LOW) * (scale * (-0.5 / CODE_LOW))
    return jnp.where(code < 0.0, -size, size)


def pack_kernel(hold_ref, key_ref, value_ref, long_ref, out_ref, stage_ref):
    parts = (
        key_ref[...].astype(f32).T,
        value_ref[...].astype(f32).T,
        encode(long_ref[...]).T,
    )
    for place, part in enumerate(parts):
        for own in range(OWN):
            piece = part[own * BLOCKS : (own + 1) * BLOCKS]
            row = 2 * (place * OWN + own)
            stage_ref[pl.ds(row, BLOCKS, stride=SENT), :] = piece[:, :LANES]
            stage_ref[pl.ds(row + 1, BLOCKS, stride=SENT), :] = piece[:, LANES:]
    out_ref[...] = stage_ref[...].astype(bf16)
    pl.delay(hold_ref[0])


def filter_kernel(
    got_ref, taps_ref, gain_ref, outer_ref, back_ref, twist_ref, inner_ref, out_ref, stage_ref, send_ref
):
    stage_ref[...] = got_ref[...].astype(f32)
    twist_real = twist_ref[0]
    twist_imag = twist_ref[1]
    inner_high = inner_ref[0]
    inner_low = inner_ref[1]
    half = OWN * BLOCKS

    def staged(row):
        return stage_ref[pl.ds(row, BLOCKS, stride=SENT), :]

    def inner_product(value):
        high, low = split(value)
        return dot(high, inner_high) + dot(high, inner_low) + dot(low, inner_high)

    def spectrum(signal):
        high, low = split(signal)
        across = dot(outer_ref[...], jnp.concatenate([high, high, low], axis=0))
        real = []
        imag = []
        for own in range(OWN):
            piece_real = across[:BLOCKS, own * ROWS : (own + 1) * ROWS]
            piece_imag = across[BLOCKS:, own * ROWS : (own + 1) * ROWS]
            real.append(piece_real * twist_real - piece_imag * twist_imag)
            imag.append(piece_real * twist_imag + piece_imag * twist_real)
        both = inner_product(jnp.concatenate(real + imag, axis=0))
        return (
            both[:half, :ROWS] + both[half:, ROWS:],
            both[half:, :ROWS] - both[:half, ROWS:],
        )

    first_row = 4 * OWN
    long_real, long_imag = spectrum(
        decode(jnp.concatenate([staged(first_row + i) for i in range(2 * OWN)], axis=1))
    )

    lane = lax.broadcasted_iota(jnp.int32, (BLOCKS, LANES), 1)
    first = lax.broadcasted_iota(jnp.int32, (SIDE_LEN, LANES), 0) == START_ROW

    def short(branch, own):
        early = staged(2 * (branch * OWN + own))
        late = staged(2 * (branch * OWN + own) + 1)
        groups = [pltpu.roll(late[-SIDE_LEN:], 1, 0)]
        groups += [late[i : i + SIDE_LEN] for i in range(0, BLOCKS - SIDE_LEN, SIDE_LEN)]
        groups[START_GROUP] = jnp.where(first, 0.0, groups[START_GROUP])
        tap = taps_ref[branch, TAPS - 1, own]
        early_sum = tap * early
        late_sum = tap * late
        for back in range(1, TAPS):
            tap = taps_ref[branch, TAPS - 1 - back, own]
            moved_early = pltpu.roll(early, back, 1)
            moved_late = pltpu.roll(late, back, 1)
            moved_before = [
                pltpu.roll(group, back, 1)
                if i in (0, START_GROUP)
                else moved_late[(i - 1) * SIDE_LEN : i * SIDE_LEN]
                for i, group in enumerate(groups)
            ]
            moved_before = jnp.concatenate(moved_before, axis=0)
            early_sum = early_sum + tap * jnp.where(lane < back, moved_before, moved_early)
            late_sum = late_sum + tap * jnp.where(lane < back, moved_early, moved_late)
        return early_sum, late_sum

    gated = []
    for own in range(OWN):
        for key_mix, value_mix in zip(short(0, own), short(1, own)):
            gated.append(key_mix * value_mix)
    signal_real, signal_imag = spectrum(jnp.concatenate(gated, axis=1))
    prod_real = signal_real * long_real - signal_imag * long_imag
    prod_imag = signal_real * long_imag + signal_imag * long_real
    both = inner_product(jnp.concatenate([prod_real, prod_imag], axis=0))
    time_real = both[:half, :ROWS] - both[half:, ROWS:]
    time_imag = both[half:, :ROWS] + both[:half, ROWS:]
    real = []
    imag = []
    for own in range(OWN):
        piece_real = time_real[own * BLOCKS : (own + 1) * BLOCKS]
        piece_imag = time_imag[own * BLOCKS : (own + 1) * BLOCKS]
        real.append(piece_real * twist_real + piece_imag * twist_imag)
        imag.append(piece_imag * twist_real - piece_real * twist_imag)
    high, low = split(
        jnp.concatenate([jnp.concatenate(real, axis=1), jnp.concatenate(imag, axis=1)], axis=0)
    )
    mixed = dot(back_ref[...], jnp.concatenate([high, high, low], axis=0))
    lane = lax.broadcasted_iota(jnp.int32, (BLOCKS, LANES), 1)
    scales = jnp.ones((BLOCKS, LANES), f32)
    for own in range(OWN):
        total = []
        for i in (2 * own, 2 * own + 1):
            here = turned(gated[i], -TURN)
            total.append(mixed[:, i * LANES : (i + 1) * LANES] + gain_ref[own] * here)
        peak = jnp.maximum(jnp.abs(total[0]), jnp.abs(total[1]))
        scale = jnp.max(peak, axis=1, keepdims=True) * (1.0 + 2.0**-7) + 1e-30
        scale = scale.astype(bf16).astype(f32)
        scales = jnp.where(lane // (LANES // OWN) == own, scale, scales)
        for part in range(2):
            code = encode_scaled(total[part], scale)
            send_ref[pl.ds(2 * own + part, BLOCKS, stride=BACK), :] = code
    send_ref[pl.ds(2 * OWN, BLOCKS, stride=BACK), :] = scales
    send_ref[pl.ds(2 * OWN + 1, BLOCKS, stride=BACK), :] = scales
    out_ref[...] = send_ref[...].astype(bf16)


def finish_kernel(got_ref, query_ref, out_ref, stage_ref):
    stage_ref[...] = got_ref[...].astype(f32)
    scales = stage_ref[pl.ds(2 * OWN, BLOCKS, stride=BACK), :]
    rows = []
    for own in range(OWN):
        lead = own * (LANES // OWN)
        scale = scales[:, lead : lead + 1]
        parts = []
        for i in (2 * own, 2 * own + 1):
            value = decode_scaled(stage_ref[pl.ds(i, BLOCKS, stride=BACK), :], scale)
            parts.append(turned(value, TURN))
        rows.append(jnp.concatenate(parts, axis=1))
    out_ref[...] = (query_ref[...] * jnp.concatenate(rows, axis=0).T).astype(bf16)


def in_vmem(count):
    return [pl.BlockSpec(memory_space=pltpu.VMEM)] * count


def short_filter(values, rim_part, weights):
    row_count = values.shape[0]
    padded = jnp.concatenate([rim_part, values], axis=0).astype(f32)
    total = weights[0] * padded[:row_count]
    for offset in range(1, weights.shape[0]):
        total = total + weights[offset] * padded[offset : offset + row_count]
    return total


def near(value):
    return pltpu.with_memory_space_constraint(value, pltpu.VMEM)


def exchange(blocks, lead):
    rows = blocks.shape[0] // BLOCKS
    shape = (BLOCKS, rows, LANES) if rows % 8 == 0 else (BLOCKS, rows // 2, 2, LANES)
    moved = lax.all_to_all(
        blocks.reshape(shape),
        "seq",
        split_axis=0,
        concat_axis=0,
        axis_index_groups=[order(lead)],
        tiled=True,
    )
    return moved.reshape(blocks.shape)


def shards(query_branch, key_branch, value_branch, short_taps, long_taps, skip_gain):
    outer, outer_back, twist, inner = make_tables()
    rim = lax.ppermute(
        query_branch[-(TAPS - 1) :], "seq", [(i, i + 1) for i in range(BLOCKS - 1)]
    )
    query_mix = short_filter(query_branch, rim, short_taps[0])
    hold = jnp.full((1,), HOLD * (1 - lax.axis_index("ch") % 2), jnp.int32)
    packed = pl.pallas_call(
        pack_kernel,
        out_shape=pltpu.VMEM((BLOCKS * SENT, LANES), bf16),
        in_specs=[pl.BlockSpec(memory_space=pltpu.SMEM)] + in_vmem(3),
        out_specs=in_vmem(1)[0],
        scratch_shapes=[pltpu.VMEM((BLOCKS * SENT, LANES), f32)],
        name="pack",
    )(hold, key_branch, value_branch, long_taps)
    got = exchange(packed, LEAD)
    got, query_mix = lax.optimization_barrier((got, query_mix))
    place = (lax.axis_index("seq") + BLOCKS - LEAD) % BLOCKS
    place = place % SIDE_LEN * SIDE_LEN + place // SIDE_LEN
    own_taps = lax.dynamic_index_in_dim(
        short_taps[1:].reshape(2, TAPS, OWN, BLOCKS), place, 3, keepdims=False
    )
    own_gain = lax.dynamic_index_in_dim(skip_gain.reshape(OWN, BLOCKS), place, 1, keepdims=False)
    mixed = pl.pallas_call(
        filter_kernel,
        out_shape=pltpu.VMEM((BLOCKS * BACK, LANES), bf16),
        in_specs=in_vmem(1) + [pl.BlockSpec(memory_space=pltpu.SMEM)] * 2 + in_vmem(4),
        out_specs=in_vmem(1)[0],
        scratch_shapes=[
            pltpu.VMEM((BLOCKS * SENT, LANES), f32),
            pltpu.VMEM((BLOCKS * BACK, LANES), f32),
        ],
        name="filter",
    )(near(got), own_taps, own_gain, near(outer), near(outer_back), near(twist), near(inner))
    back = exchange(mixed, LEAD_BACK)
    return pl.pallas_call(
        finish_kernel,
        out_shape=jax.ShapeDtypeStruct(query_branch.shape, bf16),
        in_specs=in_vmem(2),
        out_specs=in_vmem(1)[0],
        scratch_shapes=[pltpu.VMEM((BLOCKS * BACK, LANES), f32)],
        name="finish",
    )(near(back), near(query_mix))


def solution(mesh):
    return jax.shard_map(
        shards,
        mesh=mesh,
        in_specs=(
            P("seq", "ch"),
            P("seq", "ch"),
            P("seq", "ch"),
            P(None, None, "ch"),
            P("seq", "ch"),
            P("ch"),
        ),
        out_specs=P("seq", "ch"),
        check_vma=False,
    )
```

```python
import jax
import jax.numpy as jnp
import numpy as np
from jax import lax
from jax.experimental import pallas as pl
from jax.experimental.pallas import tpu as pltpu
from jax.sharding import PartitionSpec as P

f32 = jnp.float32
bf16 = jnp.bfloat16

BLOCKS = 64
ROWS = 256
OWN = 4
TOTAL = BLOCKS * ROWS
TAPS = 7
LANES = ROWS // 2
SENT = 6 * OWN
BACK = 2 * OWN + 2
HOLD = 7000
SIDE_LEN = 8
LEAD = 42
LEAD_BACK = 34
TURN = (LEAD_BACK - LEAD) // SIDE_LEN % SIDE_LEN


def order(lead):
    place = [rank % SIDE_LEN * SIDE_LEN + rank // SIDE_LEN for rank in range(BLOCKS)]
    return [(at + lead) % BLOCKS for at in place]


START_GROUP = -LEAD % SIDE_LEN
START_ROW = -LEAD % BLOCKS // SIDE_LEN

FLOOR = 2.0**-10
CODE_LOW = -125.0
CODE_RATE = 250.0 / np.log2(1.0 + 1.6 / FLOOR)


def halves(table):
    high = table.astype(jnp.bfloat16)
    low = (table - high.astype(np.float64)).astype(jnp.bfloat16)
    return high, low


def make_tables():
    turn = 2.0 * np.pi
    freq = np.arange(BLOCKS) + 0.25
    row = np.arange(ROWS)
    angle = turn * freq[:, None] * np.array(order(LEAD))[None, :] / BLOCKS
    high, low = halves(np.concatenate([np.cos(angle), -np.sin(angle)], axis=0))
    outer = np.concatenate([high, low, high], axis=1)
    angle = turn * freq[:, None] * np.array(order(LEAD_BACK))[None, :] / BLOCKS
    high, low = halves(np.concatenate([np.cos(angle.T), -np.sin(angle.T)], axis=1) / TOTAL)
    outer_back = np.concatenate([high, low, high], axis=1)
    angle = turn * freq[:, None] * row[None, :] / TOTAL
    twist = np.stack([np.cos(angle), -np.sin(angle)]).astype(np.float32)
    angle = turn * (row[:, None] * row[None, :] % ROWS) / ROWS
    inner = np.stack(halves(np.concatenate([np.cos(angle), np.sin(angle)], axis=1)))
    return outer, outer_back, twist, inner


def split(value):
    high = value.astype(bf16)
    return high, (value - high.astype(f32)).astype(bf16)


def turned(value, shift):
    groups = value.reshape(BLOCKS // SIDE_LEN, SIDE_LEN, LANES)
    return pltpu.roll(groups, shift % SIDE_LEN, 1).reshape(BLOCKS, LANES)


def dot(left, right):
    return jnp.dot(left, right, preferred_element_type=f32)


def encode(value):
    code = jnp.exp2(CODE_RATE * jnp.log2(1.0 + jnp.abs(value) * (1.0 / FLOOR)) + CODE_LOW)
    return jnp.where(value < 0.0, -code, code)


def decode(code):
    size = (jnp.exp2((jnp.log2(jnp.abs(code)) - CODE_LOW) * (1.0 / CODE_RATE)) - 1.0) * FLOOR
    return jnp.where(code < 0.0, -size, size)


def encode_scaled(value, scale):
    code = jnp.exp2(jnp.abs(value) * (-2.0 * CODE_LOW / scale) + CODE_LOW)
    return jnp.where(value < 0.0, -code, code)


def decode_scaled(code, scale):
    size = (jnp.log2(jnp.abs(code)) - CODE_LOW) * (scale * (-0.5 / CODE_LOW))
    return jnp.where(code < 0.0, -size, size)


def pack_kernel(hold_ref, key_ref, value_ref, long_ref, out_ref, stage_ref):
    parts = (
        key_ref[...].astype(f32).T,
        value_ref[...].astype(f32).T,
        encode(long_ref[...]).T,
    )
    for place, part in enumerate(parts):
        for own in range(OWN):
            piece = part[own * BLOCKS : (own + 1) * BLOCKS]
            row = 2 * (place * OWN + own)
            stage_ref[pl.ds(row, BLOCKS, stride=SENT), :] = piece[:, :LANES]
            stage_ref[pl.ds(row + 1, BLOCKS, stride=SENT), :] = piece[:, LANES:]
    out_ref[...] = stage_ref[...].astype(bf16)
    pl.delay(hold_ref[0])


def filter_kernel(
    got_ref, taps_ref, gain_ref, outer_ref, back_ref, twist_ref, inner_ref, out_ref, stage_ref, send_ref
):
    stage_ref[...] = got_ref[...].astype(f32)
    twist_real = twist_ref[0]
    twist_imag = twist_ref[1]
    inner_high = inner_ref[0]
    inner_low = inner_ref[1]
    inner_all = jnp.concatenate([inner_high, inner_low, inner_high], axis=0)
    half = OWN * BLOCKS

    def staged(row):
        return stage_ref[pl.ds(row, BLOCKS, stride=SENT), :]

    def inner_product(value):
        parts = []
        for i in range(2):
            high, low = split(value[i * half : (i + 1) * half])
            parts.append(dot(jnp.concatenate([high, high, low], axis=1), inner_all))
        return jnp.concatenate(parts, axis=0)

    def spectrum(signal):
        high, low = split(signal)
        across = dot(outer_ref[...], jnp.concatenate([high, high, low], axis=0))
        real = []
        imag = []
        for own in range(OWN):
            piece_real = across[:BLOCKS, own * ROWS : (own + 1) * ROWS]
            piece_imag = across[BLOCKS:, own * ROWS : (own + 1) * ROWS]
            real.append(piece_real * twist_real - piece_imag * twist_imag)
            imag.append(piece_real * twist_imag + piece_imag * twist_real)
        both = inner_product(jnp.concatenate(real + imag, axis=0))
        return (
            both[:half, :ROWS] + both[half:, ROWS:],
            both[half:, :ROWS] - both[:half, ROWS:],
        )

    first_row = 4 * OWN
    long_real, long_imag = spectrum(
        decode(jnp.concatenate([staged(first_row + i) for i in range(2 * OWN)], axis=1))
    )

    lane = lax.broadcasted_iota(jnp.int32, (BLOCKS, LANES), 1)
    first = lax.broadcasted_iota(jnp.int32, (SIDE_LEN, LANES), 0) == START_ROW

    def short(branch, own):
        early = staged(2 * (branch * OWN + own))
        late = staged(2 * (branch * OWN + own) + 1)
        groups = [pltpu.roll(late[-SIDE_LEN:], 1, 0)]
        groups += [late[i : i + SIDE_LEN] for i in range(0, BLOCKS - SIDE_LEN, SIDE_LEN)]
        groups[START_GROUP] = jnp.where(first, 0.0, groups[START_GROUP])
        tap = taps_ref[branch, TAPS - 1, own]
        early_sum = tap * early
        late_sum = tap * late
        for back in range(1, TAPS):
            tap = taps_ref[branch, TAPS - 1 - back, own]
            moved_early = pltpu.roll(early, back, 1)
            moved_late = pltpu.roll(late, back, 1)
            moved_before = [
                pltpu.roll(group, back, 1)
                if i in (0, START_GROUP)
                else moved_late[(i - 1) * SIDE_LEN : i * SIDE_LEN]
                for i, group in enumerate(groups)
            ]
            moved_before = jnp.concatenate(moved_before, axis=0)
            early_sum = early_sum + tap * jnp.where(lane < back, moved_before, moved_early)
            late_sum = late_sum + tap * jnp.where(lane < back, moved_early, moved_late)
        return early_sum, late_sum

    gated = []
    for own in range(OWN):
        for key_mix, value_mix in zip(short(0, own), short(1, own)):
            gated.append(key_mix * value_mix)
    signal_real, signal_imag = spectrum(jnp.concatenate(gated, axis=1))
    prod_real = signal_real * long_real - signal_imag * long_imag
    prod_imag = signal_real * long_imag + signal_imag * long_real
    both = inner_product(jnp.concatenate([prod_real, prod_imag], axis=0))
    time_real = both[:half, :ROWS] - both[half:, ROWS:]
    time_imag = both[half:, :ROWS] + both[:half, ROWS:]
    real = []
    imag = []
    for own in range(OWN):
        piece_real = time_real[own * BLOCKS : (own + 1) * BLOCKS]
        piece_imag = time_imag[own * BLOCKS : (own + 1) * BLOCKS]
        real.append(piece_real * twist_real + piece_imag * twist_imag)
        imag.append(piece_imag * twist_real - piece_real * twist_imag)
    high, low = split(
        jnp.concatenate([jnp.concatenate(real, axis=1), jnp.concatenate(imag, axis=1)], axis=0)
    )
    mixed = dot(back_ref[...], jnp.concatenate([high, high, low], axis=0))
    lane = lax.broadcasted_iota(jnp.int32, (BLOCKS, LANES), 1)
    scales = jnp.ones((BLOCKS, LANES), f32)
    for own in range(OWN):
        total = []
        for i in (2 * own, 2 * own + 1):
            here = turned(gated[i], -TURN)
            total.append(mixed[:, i * LANES : (i + 1) * LANES] + gain_ref[own] * here)
        peak = jnp.maximum(jnp.abs(total[0]), jnp.abs(total[1]))
        scale = jnp.max(peak, axis=1, keepdims=True) * (1.0 + 2.0**-7) + 1e-30
        scale = scale.astype(bf16).astype(f32)
        scales = jnp.where(lane // (LANES // OWN) == own, scale, scales)
        for part in range(2):
            code = encode_scaled(total[part], scale)
            send_ref[pl.ds(2 * own + part, BLOCKS, stride=BACK), :] = code
    send_ref[pl.ds(2 * OWN, BLOCKS, stride=BACK), :] = scales
    send_ref[pl.ds(2 * OWN + 1, BLOCKS, stride=BACK), :] = scales
    out_ref[...] = send_ref[...].astype(bf16)


def finish_kernel(got_ref, query_ref, out_ref, stage_ref):
    stage_ref[...] = got_ref[...].astype(f32)
    scales = stage_ref[pl.ds(2 * OWN, BLOCKS, stride=BACK), :]
    rows = []
    for own in range(OWN):
        lead = own * (LANES // OWN)
        scale = scales[:, lead : lead + 1]
        parts = []
        for i in (2 * own, 2 * own + 1):
            value = decode_scaled(stage_ref[pl.ds(i, BLOCKS, stride=BACK), :], scale)
            parts.append(turned(value, TURN))
        rows.append(jnp.concatenate(parts, axis=1))
    out_ref[...] = (query_ref[...] * jnp.concatenate(rows, axis=0).T).astype(bf16)


def in_vmem(count):
    return [pl.BlockSpec(memory_space=pltpu.VMEM)] * count


def short_filter(values, rim_part, weights):
    row_count = values.shape[0]
    padded = jnp.concatenate([rim_part, values], axis=0).astype(f32)
    total = weights[0] * padded[:row_count]
    for offset in range(1, weights.shape[0]):
        total = total + weights[offset] * padded[offset : offset + row_count]
    return total


def near(value):
    return pltpu.with_memory_space_constraint(value, pltpu.VMEM)


def exchange(blocks, lead):
    rows = blocks.shape[0] // BLOCKS
    shape = (BLOCKS, rows, LANES) if rows % 8 == 0 else (BLOCKS, rows // 2, 2, LANES)
    moved = lax.all_to_all(
        blocks.reshape(shape),
        "seq",
        split_axis=0,
        concat_axis=0,
        axis_index_groups=[order(lead)],
        tiled=True,
    )
    return moved.reshape(blocks.shape)


def shards(query_branch, key_branch, value_branch, short_taps, long_taps, skip_gain):
    outer, outer_back, twist, inner = make_tables()
    rim = lax.ppermute(
        query_branch[-(TAPS - 1) :], "seq", [(i, i + 1) for i in range(BLOCKS - 1)]
    )
    query_mix = short_filter(query_branch, rim, short_taps[0])
    hold = jnp.full((1,), HOLD * (1 - lax.axis_index("ch") % 2), jnp.int32)
    packed = pl.pallas_call(
        pack_kernel,
        out_shape=pltpu.VMEM((BLOCKS * SENT, LANES), bf16),
        in_specs=[pl.BlockSpec(memory_space=pltpu.SMEM)] + in_vmem(3),
        out_specs=in_vmem(1)[0],
        scratch_shapes=[pltpu.VMEM((BLOCKS * SENT, LANES), f32)],
        name="pack",
    )(hold, key_branch, value_branch, long_taps)
    got = exchange(packed, LEAD)
    got, query_mix = lax.optimization_barrier((got, query_mix))
    place = (lax.axis_index("seq") + BLOCKS - LEAD) % BLOCKS
    place = place % SIDE_LEN * SIDE_LEN + place // SIDE_LEN
    own_taps = lax.dynamic_index_in_dim(
        short_taps[1:].reshape(2, TAPS, OWN, BLOCKS), place, 3, keepdims=False
    )
    own_gain = lax.dynamic_index_in_dim(skip_gain.reshape(OWN, BLOCKS), place, 1, keepdims=False)
    mixed = pl.pallas_call(
        filter_kernel,
        out_shape=pltpu.VMEM((BLOCKS * BACK, LANES), bf16),
        in_specs=in_vmem(1) + [pl.BlockSpec(memory_space=pltpu.SMEM)] * 2 + in_vmem(4),
        out_specs=in_vmem(1)[0],
        scratch_shapes=[
            pltpu.VMEM((BLOCKS * SENT, LANES), f32),
            pltpu.VMEM((BLOCKS * BACK, LANES), f32),
        ],
        name="filter",
    )(near(got), own_taps, own_gain, near(outer), near(outer_back), near(twist), near(inner))
    back = exchange(mixed, LEAD_BACK)
    return pl.pallas_call(
        finish_kernel,
        out_shape=jax.ShapeDtypeStruct(query_branch.shape, bf16),
        in_specs=in_vmem(2),
        out_specs=in_vmem(1)[0],
        scratch_shapes=[pltpu.VMEM((BLOCKS * BACK, LANES), f32)],
        name="finish",
    )(near(back), near(query_mix))


def solution(mesh):
    return jax.shard_map(
        shards,
        mesh=mesh,
        in_specs=(
            P("seq", "ch"),
            P("seq", "ch"),
            P("seq", "ch"),
            P(None, None, "ch"),
            P("seq", "ch"),
            P("ch"),
        ),
        out_specs=P("seq", "ch"),
        check_vma=False,
    )
```

```python
import jax
import jax.numpy as jnp
import numpy as np
from jax import lax
from jax.experimental import pallas as pl
from jax.experimental.pallas import tpu as pltpu
from jax.sharding import PartitionSpec as P

f32 = jnp.float32
bf16 = jnp.bfloat16

BLOCKS = 64
ROWS = 256
OWN = 4
TOTAL = BLOCKS * ROWS
TAPS = 7
LANES = ROWS // 2
SENT = 6 * OWN
BACK = 2 * OWN + 2
HOLD = 7000
SIDE_LEN = 8
LEAD = 42
LEAD_BACK = 34
TURN = (LEAD_BACK - LEAD) // SIDE_LEN % SIDE_LEN


def order(lead):
    place = [rank % SIDE_LEN * SIDE_LEN + rank // SIDE_LEN for rank in range(BLOCKS)]
    return [(at + lead) % BLOCKS for at in place]


START_GROUP = -LEAD % SIDE_LEN
START_ROW = -LEAD % BLOCKS // SIDE_LEN

FLOOR = 2.0**-9
CODE_LOW = -125.0
CODE_RATE = 250.0 / np.log2(1.0 + 1.55 / FLOOR)


def halves(table):
    high = table.astype(jnp.bfloat16)
    low = (table - high.astype(np.float64)).astype(jnp.bfloat16)
    return high, low


def make_tables():
    turn = 2.0 * np.pi
    freq = np.arange(BLOCKS) + 0.25
    row = np.arange(ROWS)
    angle = turn * freq[:, None] * np.array(order(LEAD))[None, :] / BLOCKS
    high, low = halves(np.concatenate([np.cos(angle), -np.sin(angle)], axis=0))
    outer = np.concatenate([high, low, high], axis=1)
    angle = turn * freq[:, None] * np.array(order(LEAD_BACK))[None, :] / BLOCKS
    high, low = halves(np.concatenate([np.cos(angle.T), -np.sin(angle.T)], axis=1) / TOTAL)
    outer_back = np.concatenate([high, low, high], axis=1)
    angle = turn * freq[:, None] * row[None, :] / TOTAL
    twist = np.stack([np.cos(angle), -np.sin(angle)]).astype(np.float32)
    angle = turn * (row[:, None] * row[None, :] % ROWS) / ROWS
    inner = np.stack(halves(np.concatenate([np.cos(angle), np.sin(angle)], axis=1)))
    return outer, outer_back, twist, inner


def split(value):
    high = value.astype(bf16)
    return high, (value - high.astype(f32)).astype(bf16)


def turned(value, shift):
    groups = value.reshape(BLOCKS // SIDE_LEN, SIDE_LEN, LANES)
    return pltpu.roll(groups, shift % SIDE_LEN, 1).reshape(BLOCKS, LANES)


def dot(left, right):
    return jnp.dot(left, right, preferred_element_type=f32)


def encode(value):
    code = jnp.exp2(CODE_RATE * jnp.log2(1.0 + jnp.abs(value) * (1.0 / FLOOR)) + CODE_LOW)
    return jnp.where(value < 0.0, -code, code)


def decode(code):
    size = (jnp.exp2((jnp.log2(jnp.abs(code)) - CODE_LOW) * (1.0 / CODE_RATE)) - 1.0) * FLOOR
    return jnp.where(code < 0.0, -size, size)


def encode_scaled(value, scale):
    code = jnp.exp2(jnp.abs(value) * (-2.0 * CODE_LOW / scale) + CODE_LOW)
    return jnp.where(value < 0.0, -code, code)


def decode_scaled(code, scale):
    size = (jnp.log2(jnp.abs(code)) - CODE_LOW) * (scale * (-0.5 / CODE_LOW))
    return jnp.where(code < 0.0, -size, size)


def pack_kernel(hold_ref, key_ref, value_ref, long_ref, out_ref, stage_ref):
    parts = (
        key_ref[...].astype(f32).T,
        value_ref[...].astype(f32).T,
        encode(long_ref[...]).T,
    )
    for place, part in enumerate(parts):
        for own in range(OWN):
            piece = part[own * BLOCKS : (own + 1) * BLOCKS]
            row = 2 * (place * OWN + own)
            stage_ref[pl.ds(row, BLOCKS, stride=SENT), :] = piece[:, :LANES]
            stage_ref[pl.ds(row + 1, BLOCKS, stride=SENT), :] = piece[:, LANES:]
    out_ref[...] = stage_ref[...].astype(bf16)
    pl.delay(hold_ref[0])


def filter_kernel(
    got_ref, taps_ref, gain_ref, outer_ref, back_ref, twist_ref, inner_ref, out_ref, stage_ref, send_ref
):
    stage_ref[...] = got_ref[...].astype(f32)
    twist_real = twist_ref[0]
    twist_imag = twist_ref[1]
    inner_high = inner_ref[0]
    inner_low = inner_ref[1]
    inner_all = jnp.concatenate([inner_high, inner_low, inner_high], axis=0)
    half = OWN * BLOCKS

    def staged(row):
        return stage_ref[pl.ds(row, BLOCKS, stride=SENT), :]

    def inner_product(value):
        parts = []
        for i in range(2):
            high, low = split(value[i * half : (i + 1) * half])
            parts.append(dot(jnp.concatenate([high, high, low], axis=1), inner_all))
        return jnp.concatenate(parts, axis=0)

    def spectrum(signal):
        high, low = split(signal)
        across = dot(outer_ref[...], jnp.concatenate([high, high, low], axis=0))
        real = []
        imag = []
        for own in range(OWN):
            piece_real = across[:BLOCKS, own * ROWS : (own + 1) * ROWS]
            piece_imag = across[BLOCKS:, own * ROWS : (own + 1) * ROWS]
            real.append(piece_real * twist_real - piece_imag * twist_imag)
            imag.append(piece_real * twist_imag + piece_imag * twist_real)
        both = inner_product(jnp.concatenate(real + imag, axis=0))
        return (
            both[:half, :ROWS] + both[half:, ROWS:],
            both[half:, :ROWS] - both[:half, ROWS:],
        )

    first_row = 4 * OWN
    long_real, long_imag = spectrum(
        decode(jnp.concatenate([staged(first_row + i) for i in range(2 * OWN)], axis=1))
    )

    lane = lax.broadcasted_iota(jnp.int32, (BLOCKS, LANES), 1)
    first = lax.broadcasted_iota(jnp.int32, (SIDE_LEN, LANES), 0) == START_ROW

    def short(branch, own):
        early = staged(2 * (branch * OWN + own))
        late = staged(2 * (branch * OWN + own) + 1)
        groups = [pltpu.roll(late[-SIDE_LEN:], 1, 0)]
        groups += [late[i : i + SIDE_LEN] for i in range(0, BLOCKS - SIDE_LEN, SIDE_LEN)]
        groups[START_GROUP] = jnp.where(first, 0.0, groups[START_GROUP])
        tap = taps_ref[branch, TAPS - 1, own]
        early_sum = tap * early
        late_sum = tap * late
        for back in range(1, TAPS):
            tap = taps_ref[branch, TAPS - 1 - back, own]
            moved_early = pltpu.roll(early, back, 1)
            moved_late = pltpu.roll(late, back, 1)
            moved_before = [
                pltpu.roll(group, back, 1)
                if i in (0, START_GROUP)
                else moved_late[(i - 1) * SIDE_LEN : i * SIDE_LEN]
                for i, group in enumerate(groups)
            ]
            moved_before = jnp.concatenate(moved_before, axis=0)
            early_sum = early_sum + tap * jnp.where(lane < back, moved_before, moved_early)
            late_sum = late_sum + tap * jnp.where(lane < back, moved_early, moved_late)
        return early_sum, late_sum

    gated = []
    for own in range(OWN):
        for key_mix, value_mix in zip(short(0, own), short(1, own)):
            gated.append(key_mix * value_mix)
    signal_real, signal_imag = spectrum(jnp.concatenate(gated, axis=1))
    prod_real = signal_real * long_real - signal_imag * long_imag
    prod_imag = signal_real * long_imag + signal_imag * long_real
    both = inner_product(jnp.concatenate([prod_real, prod_imag], axis=0))
    time_real = both[:half, :ROWS] - both[half:, ROWS:]
    time_imag = both[half:, :ROWS] + both[:half, ROWS:]
    real = []
    imag = []
    for own in range(OWN):
        piece_real = time_real[own * BLOCKS : (own + 1) * BLOCKS]
        piece_imag = time_imag[own * BLOCKS : (own + 1) * BLOCKS]
        real.append(piece_real * twist_real + piece_imag * twist_imag)
        imag.append(piece_imag * twist_real - piece_real * twist_imag)
    high, low = split(
        jnp.concatenate([jnp.concatenate(real, axis=1), jnp.concatenate(imag, axis=1)], axis=0)
    )
    mixed = dot(back_ref[...], jnp.concatenate([high, high, low], axis=0))
    lane = lax.broadcasted_iota(jnp.int32, (BLOCKS, LANES), 1)
    scales = jnp.ones((BLOCKS, LANES), f32)
    for own in range(OWN):
        total = []
        for i in (2 * own, 2 * own + 1):
            here = turned(gated[i], -TURN)
            total.append(mixed[:, i * LANES : (i + 1) * LANES] + gain_ref[own] * here)
        peak = jnp.maximum(jnp.abs(total[0]), jnp.abs(total[1]))
        scale = jnp.max(peak, axis=1, keepdims=True) * (1.0 + 2.0**-7) + 1e-30
        scale = scale.astype(bf16).astype(f32)
        scales = jnp.where(lane // (LANES // OWN) == own, scale, scales)
        for part in range(2):
            code = encode_scaled(total[part], scale)
            send_ref[pl.ds(2 * own + part, BLOCKS, stride=BACK), :] = code
    send_ref[pl.ds(2 * OWN, BLOCKS, stride=BACK), :] = scales
    send_ref[pl.ds(2 * OWN + 1, BLOCKS, stride=BACK), :] = scales
    out_ref[...] = send_ref[...].astype(bf16)


def finish_kernel(got_ref, query_ref, out_ref, stage_ref):
    stage_ref[...] = got_ref[...].astype(f32)
    scales = stage_ref[pl.ds(2 * OWN, BLOCKS, stride=BACK), :]
    rows = []
    for own in range(OWN):
        lead = own * (LANES // OWN)
        scale = scales[:, lead : lead + 1]
        parts = []
        for i in (2 * own, 2 * own + 1):
            value = decode_scaled(stage_ref[pl.ds(i, BLOCKS, stride=BACK), :], scale)
            parts.append(turned(value, TURN))
        rows.append(jnp.concatenate(parts, axis=1))
    out_ref[...] = (query_ref[...] * jnp.concatenate(rows, axis=0).T).astype(bf16)


def in_vmem(count):
    return [pl.BlockSpec(memory_space=pltpu.VMEM)] * count


def short_filter(values, rim_part, weights):
    row_count = values.shape[0]
    padded = jnp.concatenate([rim_part, values], axis=0).astype(f32)
    total = weights[0] * padded[:row_count]
    for offset in range(1, weights.shape[0]):
        total = total + weights[offset] * padded[offset : offset + row_count]
    return total


def near(value):
    return pltpu.with_memory_space_constraint(value, pltpu.VMEM)


def exchange(blocks, lead):
    rows = blocks.shape[0] // BLOCKS
    shape = (BLOCKS, rows, LANES) if rows % 8 == 0 else (BLOCKS, rows // 2, 2, LANES)
    moved = lax.all_to_all(
        blocks.reshape(shape),
        "seq",
        split_axis=0,
        concat_axis=0,
        axis_index_groups=[order(lead)],
        tiled=True,
    )
    return moved.reshape(blocks.shape)


def shards(query_branch, key_branch, value_branch, short_taps, long_taps, skip_gain):
    outer, outer_back, twist, inner = make_tables()
    rim = lax.ppermute(
        query_branch[-(TAPS - 1) :], "seq", [(i, i + 1) for i in range(BLOCKS - 1)]
    )
    query_mix = short_filter(query_branch, rim, short_taps[0])
    hold = jnp.full((1,), HOLD * (1 - lax.axis_index("ch") % 2), jnp.int32)
    packed = pl.pallas_call(
        pack_kernel,
        out_shape=pltpu.VMEM((BLOCKS * SENT, LANES), bf16),
        in_specs=[pl.BlockSpec(memory_space=pltpu.SMEM)] + in_vmem(3),
        out_specs=in_vmem(1)[0],
        scratch_shapes=[pltpu.VMEM((BLOCKS * SENT, LANES), f32)],
        name="pack",
    )(hold, key_branch, value_branch, long_taps)
    got = exchange(packed, LEAD)
    got, query_mix = lax.optimization_barrier((got, query_mix))
    place = (lax.axis_index("seq") + BLOCKS - LEAD) % BLOCKS
    place = place % SIDE_LEN * SIDE_LEN + place // SIDE_LEN
    own_taps = lax.dynamic_index_in_dim(
        short_taps[1:].reshape(2, TAPS, OWN, BLOCKS), place, 3, keepdims=False
    )
    own_gain = lax.dynamic_index_in_dim(skip_gain.reshape(OWN, BLOCKS), place, 1, keepdims=False)
    mixed = pl.pallas_call(
        filter_kernel,
        out_shape=pltpu.VMEM((BLOCKS * BACK, LANES), bf16),
        in_specs=in_vmem(1) + [pl.BlockSpec(memory_space=pltpu.SMEM)] * 2 + in_vmem(4),
        out_specs=in_vmem(1)[0],
        scratch_shapes=[
            pltpu.VMEM((BLOCKS * SENT, LANES), f32),
            pltpu.VMEM((BLOCKS * BACK, LANES), f32),
        ],
        name="filter",
    )(near(got), own_taps, own_gain, near(outer), near(outer_back), near(twist), near(inner))
    back = exchange(mixed, LEAD_BACK)
    return pl.pallas_call(
        finish_kernel,
        out_shape=jax.ShapeDtypeStruct(query_branch.shape, bf16),
        in_specs=in_vmem(2),
        out_specs=in_vmem(1)[0],
        scratch_shapes=[pltpu.VMEM((BLOCKS * BACK, LANES), f32)],
        name="finish",
    )(near(back), near(query_mix))


def solution(mesh):
    return jax.shard_map(
        shards,
        mesh=mesh,
        in_specs=(
            P("seq", "ch"),
            P("seq", "ch"),
            P("seq", "ch"),
            P(None, None, "ch"),
            P("seq", "ch"),
            P("ch"),
        ),
        out_specs=P("seq", "ch"),
        check_vma=False,
    )
```

```python
import jax
import jax.numpy as jnp
import numpy as np
from jax import lax
from jax.experimental import pallas as pl
from jax.experimental.pallas import tpu as pltpu
from jax.sharding import PartitionSpec as P

f32 = jnp.float32
bf16 = jnp.bfloat16

BLOCKS = 64
ROWS = 256
OWN = 4
TOTAL = BLOCKS * ROWS
TAPS = 7
LANES = ROWS // 2
SENT = 6 * OWN
BACK = 2 * OWN + 2
HOLD = 6000
SIDE_LEN = 8
LEAD = 42
LEAD_BACK = 34
TURN = (LEAD_BACK - LEAD) // SIDE_LEN % SIDE_LEN


def order(lead):
    place = [rank % SIDE_LEN * SIDE_LEN + rank // SIDE_LEN for rank in range(BLOCKS)]
    return [(at + lead) % BLOCKS for at in place]


START_GROUP = -LEAD % SIDE_LEN
START_ROW = -LEAD % BLOCKS // SIDE_LEN

FLOOR = 2.0**-9
CODE_LOW = -125.0
CODE_RATE = 250.0 / np.log2(1.0 + 1.55 / FLOOR)


def halves(table):
    high = table.astype(jnp.bfloat16)
    low = (table - high.astype(np.float64)).astype(jnp.bfloat16)
    return high, low


def make_tables():
    turn = 2.0 * np.pi
    freq = np.arange(BLOCKS) + 0.25
    row = np.arange(ROWS)
    angle = turn * freq[:, None] * np.array(order(LEAD))[None, :] / BLOCKS
    high, low = halves(np.concatenate([np.cos(angle), -np.sin(angle)], axis=0))
    outer = np.concatenate([high, low, high], axis=1)
    angle = turn * freq[:, None] * np.array(order(LEAD_BACK))[None, :] / BLOCKS
    high, low = halves(np.concatenate([np.cos(angle.T), -np.sin(angle.T)], axis=1) / TOTAL)
    outer_back = np.concatenate([high, low, high], axis=1)
    angle = turn * freq[:, None] * row[None, :] / TOTAL
    twist = np.stack([np.cos(angle), -np.sin(angle)]).astype(np.float32)
    angle = turn * (row[:, None] * row[None, :] % ROWS) / ROWS
    inner = np.stack(halves(np.concatenate([np.cos(angle), np.sin(angle)], axis=1)))
    return outer, outer_back, twist, inner


def split(value):
    high = value.astype(bf16)
    return high, (value - high.astype(f32)).astype(bf16)


def turned(value, shift):
    groups = value.reshape(BLOCKS // SIDE_LEN, SIDE_LEN, LANES)
    return pltpu.roll(groups, shift % SIDE_LEN, 1).reshape(BLOCKS, LANES)


def dot(left, right):
    return jnp.dot(left, right, preferred_element_type=f32)


def encode(value):
    code = jnp.exp2(CODE_RATE * jnp.log2(1.0 + jnp.abs(value) * (1.0 / FLOOR)) + CODE_LOW)
    return jnp.where(value < 0.0, -code, code)


def decode(code):
    size = (jnp.exp2((jnp.log2(jnp.abs(code)) - CODE_LOW) * (1.0 / CODE_RATE)) - 1.0) * FLOOR
    return jnp.where(code < 0.0, -size, size)


def encode_scaled(value, scale):
    code = jnp.exp2(jnp.abs(value) * (-2.0 * CODE_LOW / scale) + CODE_LOW)
    return jnp.where(value < 0.0, -code, code)


def decode_scaled(code, scale):
    size = (jnp.log2(jnp.abs(code)) - CODE_LOW) * (scale * (-0.5 / CODE_LOW))
    return jnp.where(code < 0.0, -size, size)


def pack_kernel(hold_ref, key_ref, value_ref, long_ref, out_ref, stage_ref):
    parts = (
        key_ref[...].astype(f32).T,
        value_ref[...].astype(f32).T,
        encode(long_ref[...]).T,
    )
    for place, part in enumerate(parts):
        for own in range(OWN):
            piece = part[own * BLOCKS : (own + 1) * BLOCKS]
            row = 2 * (place * OWN + own)
            stage_ref[pl.ds(row, BLOCKS, stride=SENT), :] = piece[:, :LANES]
            stage_ref[pl.ds(row + 1, BLOCKS, stride=SENT), :] = piece[:, LANES:]
    out_ref[...] = stage_ref[...].astype(bf16)
    pl.delay(hold_ref[0])


def filter_kernel(
    got_ref, taps_ref, gain_ref, outer_ref, back_ref, twist_ref, inner_ref, out_ref, stage_ref, send_ref
):
    stage_ref[...] = got_ref[...].astype(f32)
    twist_real = twist_ref[0]
    twist_imag = twist_ref[1]
    inner_high = inner_ref[0]
    inner_low = inner_ref[1]
    inner_all = jnp.concatenate([inner_high, inner_low, inner_high], axis=0)
    half = OWN * BLOCKS

    def staged(row):
        return stage_ref[pl.ds(row, BLOCKS, stride=SENT), :]

    def inner_product(value):
        parts = []
        for i in range(2):
            high, low = split(value[i * half : (i + 1) * half])
            parts.append(dot(jnp.concatenate([high, high, low], axis=1), inner_all))
        return jnp.concatenate(parts, axis=0)

    def spectrum(signal):
        high, low = split(signal)
        across = dot(outer_ref[...], jnp.concatenate([high, high, low], axis=0))
        real = []
        imag = []
        for own in range(OWN):
            piece_real = across[:BLOCKS, own * ROWS : (own + 1) * ROWS]
            piece_imag = across[BLOCKS:, own * ROWS : (own + 1) * ROWS]
            real.append(piece_real * twist_real - piece_imag * twist_imag)
            imag.append(piece_real * twist_imag + piece_imag * twist_real)
        both = inner_product(jnp.concatenate(real + imag, axis=0))
        return (
            both[:half, :ROWS] + both[half:, ROWS:],
            both[half:, :ROWS] - both[:half, ROWS:],
        )

    first_row = 4 * OWN
    long_real, long_imag = spectrum(
        decode(jnp.concatenate([staged(first_row + i) for i in range(2 * OWN)], axis=1))
    )

    lane = lax.broadcasted_iota(jnp.int32, (BLOCKS, LANES), 1)
    first = lax.broadcasted_iota(jnp.int32, (SIDE_LEN, LANES), 0) == START_ROW

    def short(branch, own):
        early = staged(2 * (branch * OWN + own))
        late = staged(2 * (branch * OWN + own) + 1)
        groups = [pltpu.roll(late[-SIDE_LEN:], 1, 0)]
        groups += [late[i : i + SIDE_LEN] for i in range(0, BLOCKS - SIDE_LEN, SIDE_LEN)]
        groups[START_GROUP] = jnp.where(first, 0.0, groups[START_GROUP])
        tap = taps_ref[branch, TAPS - 1, own]
        early_sum = tap * early
        late_sum = tap * late
        for back in range(1, TAPS):
            tap = taps_ref[branch, TAPS - 1 - back, own]
            moved_early = pltpu.roll(early, back, 1)
            moved_late = pltpu.roll(late, back, 1)
            moved_before = [
                pltpu.roll(group, back, 1)
                if i in (0, START_GROUP)
                else moved_late[(i - 1) * SIDE_LEN : i * SIDE_LEN]
                for i, group in enumerate(groups)
            ]
            moved_before = jnp.concatenate(moved_before, axis=0)
            early_sum = early_sum + tap * jnp.where(lane < back, moved_before, moved_early)
            late_sum = late_sum + tap * jnp.where(lane < back, moved_early, moved_late)
        return early_sum, late_sum

    gated = []
    for own in range(OWN):
        for key_mix, value_mix in zip(short(0, own), short(1, own)):
            gated.append(key_mix * value_mix)
    signal_real, signal_imag = spectrum(jnp.concatenate(gated, axis=1))
    prod_real = signal_real * long_real - signal_imag * long_imag
    prod_imag = signal_real * long_imag + signal_imag * long_real
    both = inner_product(jnp.concatenate([prod_real, prod_imag], axis=0))
    time_real = both[:half, :ROWS] - both[half:, ROWS:]
    time_imag = both[half:, :ROWS] + both[:half, ROWS:]
    real = []
    imag = []
    for own in range(OWN):
        piece_real = time_real[own * BLOCKS : (own + 1) * BLOCKS]
        piece_imag = time_imag[own * BLOCKS : (own + 1) * BLOCKS]
        real.append(piece_real * twist_real + piece_imag * twist_imag)
        imag.append(piece_imag * twist_real - piece_real * twist_imag)
    high, low = split(
        jnp.concatenate([jnp.concatenate(real, axis=1), jnp.concatenate(imag, axis=1)], axis=0)
    )
    mixed = dot(back_ref[...], jnp.concatenate([high, high, low], axis=0))
    lane = lax.broadcasted_iota(jnp.int32, (BLOCKS, LANES), 1)
    scales = jnp.ones((BLOCKS, LANES), f32)
    for own in range(OWN):
        total = []
        for i in (2 * own, 2 * own + 1):
            here = turned(gated[i], -TURN)
            total.append(mixed[:, i * LANES : (i + 1) * LANES] + gain_ref[own] * here)
        peak = jnp.maximum(jnp.abs(total[0]), jnp.abs(total[1]))
        scale = jnp.max(peak, axis=1, keepdims=True) * (1.0 + 2.0**-7) + 1e-30
        scale = scale.astype(bf16).astype(f32)
        scales = jnp.where(lane // (LANES // OWN) == own, scale, scales)
        for part in range(2):
            code = encode_scaled(total[part], scale)
            send_ref[pl.ds(2 * own + part, BLOCKS, stride=BACK), :] = code
    send_ref[pl.ds(2 * OWN, BLOCKS, stride=BACK), :] = scales
    send_ref[pl.ds(2 * OWN + 1, BLOCKS, stride=BACK), :] = scales
    out_ref[...] = send_ref[...].astype(bf16)


def finish_kernel(got_ref, query_ref, out_ref, stage_ref):
    stage_ref[...] = got_ref[...].astype(f32)
    scales = stage_ref[pl.ds(2 * OWN, BLOCKS, stride=BACK), :]
    rows = []
    for own in range(OWN):
        lead = own * (LANES // OWN)
        scale = scales[:, lead : lead + 1]
        parts = []
        for i in (2 * own, 2 * own + 1):
            value = decode_scaled(stage_ref[pl.ds(i, BLOCKS, stride=BACK), :], scale)
            parts.append(turned(value, TURN))
        rows.append(jnp.concatenate(parts, axis=1))
    out_ref[...] = (query_ref[...] * jnp.concatenate(rows, axis=0).T).astype(bf16)


def in_vmem(count):
    return [pl.BlockSpec(memory_space=pltpu.VMEM)] * count


def short_filter(values, rim_part, weights):
    row_count = values.shape[0]
    padded = jnp.concatenate([rim_part, values], axis=0).astype(f32)
    total = weights[0] * padded[:row_count]
    for offset in range(1, weights.shape[0]):
        total = total + weights[offset] * padded[offset : offset + row_count]
    return total


def near(value):
    return pltpu.with_memory_space_constraint(value, pltpu.VMEM)


def exchange(blocks, lead):
    rows = blocks.shape[0] // BLOCKS
    shape = (BLOCKS, rows, LANES) if rows % 8 == 0 else (BLOCKS, rows // 2, 2, LANES)
    moved = lax.all_to_all(
        blocks.reshape(shape),
        "seq",
        split_axis=0,
        concat_axis=0,
        axis_index_groups=[order(lead)],
        tiled=True,
    )
    return moved.reshape(blocks.shape)


def shards(query_branch, key_branch, value_branch, short_taps, long_taps, skip_gain):
    outer, outer_back, twist, inner = make_tables()
    rim = lax.ppermute(
        query_branch[-(TAPS - 1) :], "seq", [(i, i + 1) for i in range(BLOCKS - 1)]
    )
    query_mix = short_filter(query_branch, rim, short_taps[0])
    hold = jnp.full((1,), HOLD * (1 - lax.axis_index("ch") % 2), jnp.int32)
    packed = pl.pallas_call(
        pack_kernel,
        out_shape=pltpu.VMEM((BLOCKS * SENT, LANES), bf16),
        in_specs=[pl.BlockSpec(memory_space=pltpu.SMEM)] + in_vmem(3),
        out_specs=in_vmem(1)[0],
        scratch_shapes=[pltpu.VMEM((BLOCKS * SENT, LANES), f32)],
        name="pack",
    )(hold, key_branch, value_branch, long_taps)
    got = exchange(packed, LEAD)
    got, query_mix = lax.optimization_barrier((got, query_mix))
    place = (lax.axis_index("seq") + BLOCKS - LEAD) % BLOCKS
    place = place % SIDE_LEN * SIDE_LEN + place // SIDE_LEN
    own_taps = lax.dynamic_index_in_dim(
        short_taps[1:].reshape(2, TAPS, OWN, BLOCKS), place, 3, keepdims=False
    )
    own_gain = lax.dynamic_index_in_dim(skip_gain.reshape(OWN, BLOCKS), place, 1, keepdims=False)
    mixed = pl.pallas_call(
        filter_kernel,
        out_shape=pltpu.VMEM((BLOCKS * BACK, LANES), bf16),
        in_specs=in_vmem(1) + [pl.BlockSpec(memory_space=pltpu.SMEM)] * 2 + in_vmem(4),
        out_specs=in_vmem(1)[0],
        scratch_shapes=[
            pltpu.VMEM((BLOCKS * SENT, LANES), f32),
            pltpu.VMEM((BLOCKS * BACK, LANES), f32),
        ],
        name="filter",
    )(near(got), own_taps, own_gain, near(outer), near(outer_back), near(twist), near(inner))
    back = exchange(mixed, LEAD_BACK)
    return pl.pallas_call(
        finish_kernel,
        out_shape=jax.ShapeDtypeStruct(query_branch.shape, bf16),
        in_specs=in_vmem(2),
        out_specs=in_vmem(1)[0],
        scratch_shapes=[pltpu.VMEM((BLOCKS * BACK, LANES), f32)],
        name="finish",
    )(near(back), near(query_mix))


def solution(mesh):
    return jax.shard_map(
        shards,
        mesh=mesh,
        in_specs=(
            P("seq", "ch"),
            P("seq", "ch"),
            P("seq", "ch"),
            P(None, None, "ch"),
            P("seq", "ch"),
            P("ch"),
        ),
        out_specs=P("seq", "ch"),
        check_vma=False,
    )
```
